32 devices in a mesh: groups: 2 (over y), dp: 4 (over z), tensor: 4 (over x, core).
Axes of the slice: x: 2, y: 2, z: 4, core: 2. Of those that a mesh axis runs over, the one named last changes fastest.
Arguments:
- feature_cache: bfloat16 [512, 8, 3, 8192], P(('groups', 'dp'), None, None, 'tensor'), parts along dimension 0
- owner_ids: int32 [512, 1], P(('groups', 'dp')), parts along dimension 0, may hold values from 0 to 3; in each aligned block of 64 rows (0 to 63, 64 to 127, ...) at most 24 rows name the same one
- slot_ids: int32 [512], P(('groups', 'dp')), parts along dimension 0, may hold values from 0 to 63
- live_tokens: int32 [512], P(('groups', 'dp')), parts along dimension 0, may hold values from 1 to 8
- tap_gain: float32 [3, 8192], P(None, 'tensor'), may hold values from 0.1 to 1.9
- key_cotangent: bfloat16 [4096, 1024], P(('groups', 'dp'), 'tensor'), parts along dimension 0, may hold values from -0.1875 to 0.1875
- value_cotangent: bfloat16 [4096, 1024], P(('groups', 'dp'), 'tensor'), parts along dimension 0, may hold values from -0.1875 to 0.1875
Outputs:
- kv_gradient: float32 [4096, 8192], P(('groups', 'dp'), 'tensor'), parts along dimension 0
The draws below stay inside these ranges and needn't reach their ends.
There are 2 independent parts, one for each index of `groups`. The reference program is written for one: setup_inputs(seed, part) draws one part's arguments, and reference() takes and returns one part's arrays. A program takes and returns all parts, laid end to end along the dimension named above; an argument that names none is the same for every part. Nothing has to cross between parts.
Inputs may be any that keep to these rules, and one draw needn't show every extreme that they name: `owner_ids`: among the 64 entries of one device's list, no owner is named more than 24 times, a bound that some block reaches.
All inputs are finite; a program needn't handle non-finite values.
Results may differ from the reference program's by a relative error of at most 0.009.
Values may be sent and summed in bfloat16 or wider, within the bound.
A program may use at most 128 MiB of HBM per device.

```python
import math
import jax
import jax.numpy as jnp
import numpy as np
from jax import lax

D = 8192
KV_HEADS = 8
HEAD = 128
TAPS = 3
BLOCK = 8
TOK_DEV = 512
FETCH = 64
CAP = 24
BLOCKS = 256
TOKENS = 2048
N_DP = 4


def draw_feature_cache(key, part):
    key_noise, key_column, key_row = jax.random.split(key, 3)
    full_shape = (BLOCKS, BLOCK, TAPS, D)
    column = jnp.arange(D, dtype=jnp.float32) / D
    noise = jax.random.normal(key_noise, full_shape, jnp.float32)
    column_scale = 10.0 ** column * jax.random.uniform(key_column, (D,), jnp.float32, 0.7, 1.3)
    row_scale = 10.0 ** jax.random.uniform(key_row, (BLOCKS, BLOCK, TAPS, 1), jnp.float32, 0.0, 1.0)
    return (noise * column_scale * row_scale).astype(jnp.bfloat16)


def touch_ends(values, rng, least, largest):
    longest = values.shape.index(max(values.shape))
    spots = []
    for shift in (0, 1):
        where = [jax.random.randint(jax.random.fold_in(rng, axis), (), 0, length) for axis, length in enumerate(values.shape)]
        where[longest] = (where[longest] + shift) % values.shape[longest]
        spots.append(tuple(where))
    return values.at[spots[0]].set(least).at[spots[1]].set(largest)


def spiked(drawn, key, source, target, shards_of, factor):
    def block_of(axis_at):
        return (jnp.arange(drawn.shape[axis_at]) // (drawn.shape[axis_at] // shards_of)).reshape((-1,) + (1,) * (drawn.ndim - 1 - axis_at))

    one_side = jax.random.permutation(key, shards_of)[block_of(target)]
    second = (block_of(target) + shards_of // 2) % shards_of
    return jnp.where((block_of(source) == one_side) | (block_of(source) == second), factor * drawn, drawn)


def steps_of(rng, shape, cuts, low, high):
    loudness, own = 1.0, jax.random.fold_in(rng, 6)
    for axis_at, blocks in cuts:
        heights = jnp.exp(jax.random.uniform(jax.random.fold_in(own, axis_at), (blocks,), jnp.float32, low / len(cuts), high / len(cuts)))
        loudness = loudness * jnp.repeat(heights, shape[axis_at] // blocks).reshape([-1 if axis == axis_at else 1 for axis in range(len(shape))])
    return loudness


def deal_out(stream_key, own, number, rows, count, top, bound, skew):
    order = jax.random.permutation(stream_key, count)
    heavy_load, common = portions_of(count, rows * top, bound, skew, True), portions_of(count, rows * top, bound, skew, False)
    places = jnp.arange(count)

    def named(tallies, turn):
        used = int((tallies > 0).sum())
        fixed = max(1, used // 4)
        passed = fixed + (places - fixed + turn * (used - fixed)) % max(1, count - fixed)
        return jnp.zeros((count,), jnp.int32).at[order[jnp.where(places < fixed, places, passed)]].set(jnp.asarray(tallies, jnp.int32))

    tallies = jnp.where(number % 4 == 0, named(heavy_load, number // 4), named(common, number - number // 4 - 1))
    mixed = jax.random.permutation(jax.random.fold_in(own, 3), count)
    source_of, sink = mixed[0:count // 2 * 2:2], mixed[1:count // 2 * 2:2]
    margin = jnp.minimum(tallies[source_of] - 1, bound - tallies[sink]) // 2
    margin = jnp.where((source_of == order[0]) | (sink == order[0]) | (tallies[sink] == 0), 0, jnp.maximum(margin, 0))
    passed = jax.random.randint(jax.random.fold_in(own, 4), (count // 2,), 0, 1 << 20) % (margin + 1)
    tallies = tallies.at[source_of].add(-passed).at[sink].add(passed)
    items = jnp.searchsorted(jnp.cumsum(tallies), jnp.arange(rows * top), side="right").astype(jnp.int32)
    listing = items.reshape(top, rows).T
    listing = listing[jax.random.permutation(jax.random.fold_in(own, 1), rows)]
    turn = jax.random.randint(jax.random.fold_in(own, 2), (rows, 1), 0, top)
    return jnp.take_along_axis(listing, (jnp.arange(top)[None, :] + turn) % top, axis=1)


def portions_of(amount, total, limit, skew, full):
    weights = [(1 << 20) // math.isqrt(rank ** skew) + 1 for rank in range(1, amount + 1)]
    largest = limit if full else min(limit, max(-(-total // amount), total * weights[0] // sum(weights)))
    least = 1 if total - largest >= amount - 1 else 0
    holding, spare = [largest] + [least] * (amount - 1), total - largest - least * (amount - 1)
    while spare > 0:
        free = [i for i in range(1, amount) if holding[i] < largest] or [i for i in range(1, amount) if holding[i] < limit]
        pool, budget = sum([weights[i] for i in free]), spare
        for i in free:
            addition = min(limit - holding[i], max(1, budget * weights[i] // pool), spare)
            holding[i] = holding[i] + addition
            spare = spare - addition
    return np.array(holding)


def noise_with(rng, dims, width, most, cuts, heavy, kind=jnp.bfloat16):
    drawn = width * jax.random.normal(rng, dims, jnp.float32)
    if cuts:
        drawn = drawn * steps_of(rng, dims, cuts, -0.22, 0.18)
    return jnp.clip(spiked(drawn, jax.random.fold_in(rng, 3), *heavy), -most, most).astype(kind)


def setup_inputs(seed: int = 0, part: int = 0) -> dict:
    splits = jax.random.split(jax.random.key(seed), 8)
    own_keys = jax.random.split(jax.random.fold_in(splits[7], part), 8)
    feature_cache = draw_feature_cache(jax.random.fold_in(jax.random.fold_in(splits[7], part), 71), part)
    owner_ids_keys = jax.random.split(jax.random.fold_in(own_keys[1], 1), BLOCKS // FETCH)
    owner_ids_turns = jax.random.permutation(jax.random.fold_in(own_keys[1], 3), BLOCKS // FETCH)
    owner_ids = jax.vmap(lambda own, number: deal_out(jax.random.fold_in(own_keys[1], 2), own, number, FETCH, N_DP, 1, CAP, 2))(owner_ids_keys, owner_ids_turns).reshape((BLOCKS, 1))
    slot_ids = touch_ends(jax.random.randint(own_keys[2], (BLOCKS,), 0, FETCH), jax.random.fold_in(own_keys[2], 1), 0, FETCH - 1).astype(jnp.int32)
    live_tokens = touch_ends(jax.random.randint(own_keys[3], (BLOCKS,), 1, BLOCK + 1), jax.random.fold_in(own_keys[3], 1), 1, BLOCK).astype(jnp.int32)
    tap_gain = jnp.clip(1.0 + 0.18 * jax.random.normal(splits[4], (TAPS, D), jnp.float32), 0.1, 1.9)
    key_cotangent = noise_with(own_keys[5], (TOKENS, KV_HEADS * HEAD), TOKENS ** -0.5, 0.1875, ((0, 4), (1, 4)), (0, 1, 4, 2.0))
    value_cotangent = noise_with(own_keys[6], (TOKENS, KV_HEADS * HEAD), TOKENS ** -0.5, 0.1875, ((0, 4), (1, 4)), (0, 1, 4, 2.0))
    return dict(feature_cache=feature_cache, owner_ids=owner_ids, slot_ids=slot_ids, live_tokens=live_tokens, tap_gain=tap_gain, key_cotangent=key_cotangent, value_cotangent=value_cotangent)


epsilon = 1e-06

def reference(feature_cache, owner_ids, slot_ids, live_tokens, tap_gain, key_cotangent, value_cotangent):
    block_index = (owner_ids[:, 0] * FETCH + slot_ids).astype(jnp.int32)
    cotangent = jnp.concatenate([key_cotangent, value_cotangent], axis=1)
    offsets = jnp.arange(BLOCK, dtype=jnp.int32)

    def add_shard(accumulated, step_index):
        first_block = (step_index * FETCH).astype(jnp.int32)
        chosen_ids = lax.dynamic_slice_in_dim(block_index, first_block, FETCH, 0)
        live_counts = lax.dynamic_slice_in_dim(live_tokens, first_block, FETCH, 0)
        floats = jnp.take(feature_cache, chosen_ids, axis=0).astype(jnp.float32)
        mean_square = lax.optimization_barrier(jnp.mean(floats * floats, axis=-1, keepdims=True))
        normed = floats * lax.rsqrt(mean_square + epsilon) * tap_gain
        live_mask = (offsets[None, :] < live_counts[:, None]).astype(jnp.float32)
        united = (lax.optimization_barrier(jnp.sum(normed, axis=2)) * live_mask[:, :, None]).astype(jnp.bfloat16).reshape(TOK_DEV, D)
        first_row = (step_index * TOK_DEV).astype(jnp.int32)
        grads = lax.dynamic_slice_in_dim(cotangent, first_row, TOK_DEV, 0)
        partial_value = lax.dot_general(grads, united, (((0,), (0,)), ((), ())), preferred_element_type=jnp.float32)
        partial_value = lax.optimization_barrier(partial_value.astype(jnp.bfloat16)).astype(jnp.float32)
        return (accumulated + partial_value, None)
    start_value = jnp.zeros((cotangent.shape[1], D), jnp.float32)
    kv_gradient, _ = lax.scan(add_shard, start_value, jnp.arange(N_DP, dtype=jnp.int32))
    return kv_gradient
```

```python
import jax
import jax.numpy as jnp
from jax import lax
from jax.sharding import PartitionSpec as P

EPSILON = 1e-06


def united_of(feature_cache, tap_gain, width):
    floats = feature_cache.astype(jnp.float32)
    squares = lax.psum(jnp.sum(floats * floats, axis=-1), "tensor")
    inverse_rms = lax.rsqrt(squares / width + EPSILON)
    return jnp.sum(floats * inverse_rms[..., None] * tap_gain, axis=2).astype(jnp.bfloat16)


def slot_matrix(owner_ids, slot_ids, live_tokens, owned, dtype):
    index = owner_ids[:, 0] * owned + slot_ids
    table = lax.all_gather(jnp.stack([index, live_tokens]), "dp", axis=1, tiled=True)
    slots = lax.axis_size("dp") * owned
    chosen = jnp.arange(slots, dtype=jnp.int32)[:, None] == table[0][None, :]
    return chosen.astype(dtype), table[1]


def body(feature_cache, owner_ids, slot_ids, live_tokens, tap_gain, key_cotangent, value_cotangent):
    owned, block_len, _, columns = feature_cache.shape
    width = columns * lax.axis_size("tensor")
    united = united_of(feature_cache, tap_gain, width).reshape(owned * block_len, columns)
    everywhere = lax.all_gather(united, "dp", axis=0, tiled=True)
    chosen, live = slot_matrix(owner_ids, slot_ids, live_tokens, owned, jnp.bfloat16)
    joined = jnp.concatenate(
        [
            lax.all_gather(key_cotangent, "tensor", axis=1, tiled=True),
            lax.all_gather(value_cotangent, "tensor", axis=1, tiled=True),
        ],
        axis=1,
    )
    mine = lax.all_to_all(joined, "dp", split_axis=1, concat_axis=0, tiled=True)
    rows = mine.shape[1]
    mine = mine.reshape(-1, block_len, rows)
    mask = jnp.arange(block_len, dtype=jnp.int32)[None, :] < live[:, None]
    mine = jnp.where(mask[:, :, None], mine, jnp.zeros_like(mine)).reshape(-1, block_len * rows)
    by_slot = lax.dot_general(
        chosen, mine, (((1,), (0,)), ((), ())), preferred_element_type=jnp.float32
    ).astype(jnp.bfloat16).reshape(-1, rows)
    return lax.dot_general(
        by_slot, everywhere, (((0,), (0,)), ((), ())), preferred_element_type=jnp.float32
    )


def solution(mesh):
    in_specs = (
        P(("groups", "dp"), None, None, "tensor"),
        P(("groups", "dp"), None),
        P(("groups", "dp")),
        P(("groups", "dp")),
        P(None, "tensor"),
        P(("groups", "dp"), "tensor"),
        P(("groups", "dp"), "tensor"),
    )
    out_specs = P(("groups", "dp"), "tensor")
    return jax.shard_map(body, mesh=mesh, in_specs=in_specs, out_specs=out_specs, check_vma=False)
```

```python
import jax
import jax.numpy as jnp
from jax import lax
from jax.experimental import pallas as pl
from jax.experimental.pallas import tpu as pltpu
from jax.sharding import PartitionSpec as P

EPSILON = 1e-06


def united_of(feature_cache, tap_gain, width):
    floats = feature_cache.astype(jnp.float32)
    squares = lax.psum(jnp.sum(floats * floats, axis=-1), "tensor")
    inverse_rms = lax.rsqrt(squares / width + EPSILON)
    return jnp.sum(floats * inverse_rms[..., None] * tap_gain, axis=2).astype(jnp.bfloat16)


def slot_matrix(owner_ids, slot_ids, live_tokens, owned, dtype):
    index = owner_ids[:, 0] * owned + slot_ids
    table = lax.all_gather(jnp.stack([index, live_tokens]), "dp", axis=1, tiled=True)
    slots = lax.axis_size("dp") * owned
    chosen = jnp.arange(slots, dtype=jnp.int32)[:, None] == table[0][None, :]
    return chosen.astype(dtype), table[1]


def general_body(feature_cache, owner_ids, slot_ids, live_tokens, tap_gain, key_cotangent, value_cotangent):
    owned, block_len, _, columns = feature_cache.shape
    width = columns * lax.axis_size("tensor")
    united = united_of(feature_cache, tap_gain, width).reshape(owned * block_len, columns)
    everywhere = lax.all_gather(united, "dp", axis=0, tiled=True)
    chosen, live = slot_matrix(owner_ids, slot_ids, live_tokens, owned, jnp.bfloat16)
    joined = jnp.concatenate(
        [
            lax.all_gather(key_cotangent, "tensor", axis=1, tiled=True),
            lax.all_gather(value_cotangent, "tensor", axis=1, tiled=True),
        ],
        axis=1,
    )
    mine = lax.all_to_all(joined, "dp", split_axis=1, concat_axis=0, tiled=True)
    rows = mine.shape[1]
    mine = mine.reshape(-1, block_len, rows)
    mask = jnp.arange(block_len, dtype=jnp.int32)[None, :] < live[:, None]
    mine = jnp.where(mask[:, :, None], mine, jnp.zeros_like(mine)).reshape(-1, block_len * rows)
    by_slot = lax.dot_general(
        chosen, mine, (((1,), (0,)), ((), ())), preferred_element_type=jnp.float32
    ).astype(jnp.bfloat16).reshape(-1, rows)
    return lax.dot_general(
        by_slot, everywhere, (((0,), (0,)), ((), ())), preferred_element_type=jnp.float32
    )


MESH = pl.DeviceIdType.MESH
CHUNK = 256


def line_kernel(
    u_in, idx_in, mine_in, near_in, mid_in, far_in, out,
    uall, cbuf, select, st, gbuf, stage, outv, idxv,
    usend, urecv, csend, crecv, gsend, grecv, osem, lsem, isend, irecv,
):
    z, c = lax.axis_index("dp"), lax.axis_index("tensor")
    tok, columns = u_in.shape
    share = mine_in.shape[1]
    chunks = columns // CHUNK
    sibling, across = c + 1 - 2 * lax.rem(c, 2), lax.rem(c + 2, 4)
    across_sibling = lax.rem(sibling + 2, 4)
    is_hub = (z == 1) | (z == 2)

    def remote(src, dst, ss, rs, dz, dc):
        return pltpu.make_async_remote_copy(
            src_ref=src, dst_ref=dst, send_sem=ss, recv_sem=rs,
            device_id={"dp": dz, "tensor": dc}, device_id_type=MESH,
        )

    def cols(j):
        return pl.ds(pl.multiple_of(j * CHUNK, CHUNK), CHUNK)

    own_u = pltpu.make_async_copy(u_in, uall.at[z], lsem.at[0])
    own_idx = pltpu.make_async_copy(idx_in, idxv.at[z], lsem.at[1])
    own_u.start()
    own_idx.start()

    barrier = pltpu.get_barrier_semaphore()
    for step in range(1, 4):
        pl.semaphore_signal(
            barrier, inc=1, device_id={"dp": lax.rem(z + step, 4), "tensor": c}, device_id_type=MESH
        )
    for peer in (sibling, across):
        pl.semaphore_signal(barrier, inc=1, device_id={"dp": z, "tensor": peer}, device_id_type=MESH)
    pl.semaphore_wait(barrier, 5)
    own_u.wait()
    own_idx.wait()

    def u_copy(owner, j, sem, dz):
        return remote(uall.at[owner, :, cols(j)], uall.at[owner, :, cols(j)], sem, urecv.at[owner, j], dz, c)

    def idx_copy(owner, sem, dz):
        return remote(idxv.at[owner], idxv.at[owner], sem, irecv.at[owner], dz, c)

    def out_copy(j):
        return pltpu.make_async_copy(outv.at[:, cols(j)], out.at[:, cols(j)], osem.at[j])

    def g_copy(j, dz):
        return remote(stage.at[:, cols(j)], gbuf.at[:, cols(j)], gsend.at[j], grecv.at[j], dz, c)

    @pl.when(jnp.logical_not(is_hub))
    def _():
        hub = 1 + z // 3
        for n, dz in enumerate((hub, 3 - hub)):
            idx_copy(z, isend.at[n], dz).start()
        for j in range(chunks):
            u_copy(z, j, usend.at[0, j], hub).start()
        for n, dz in enumerate((hub, 3 - hub)):
            idx_copy(z, isend.at[n], dz).wait_send()

        def take(j, carry):
            g_copy(j, hub).wait_recv()
            outv[:, cols(j)] = gbuf[:, cols(j)].astype(jnp.float32)
            out_copy(j).start()
            return carry

        lax.fori_loop(0, chunks, take, 0)
        for j in range(chunks):
            u_copy(z, j, usend.at[0, j], hub).wait_send()
            out_copy(j).wait()

    @pl.when(is_hub)
    def _():
        leaf, other = 3 * (z - 1), 3 - z
        far_leaf = 3 - leaf
        idx_copy(z, isend.at[0], other).start()
        places = (z, leaf, other, far_leaf)
        loads = []
        for n, (ref, place) in enumerate(zip((mine_in, near_in, mid_in, far_in), places)):
            loads.append(pltpu.make_async_copy(ref, cbuf.at[c, pl.ds(pl.multiple_of(place * tok, tok), tok)], lsem.at[2 + n]))
            loads[n].start()

        def c_copy(kind, n, who, dc):
            part = cbuf.at[who, pl.ds(pl.multiple_of(places[n] * tok, tok), tok)]
            return remote(part, part, csend.at[kind, n], crecv.at[kind, n], z, dc)

        for n in range(4):
            loads[n].wait()
            c_copy(0, n, c, across).start()
            c_copy(1, n, c, sibling).start()
        for j in range(chunks):
            u_copy(z, j, usend.at[0, j], other).start()
        for place in (leaf, other, far_leaf):
            idx_copy(place, isend.at[0], other).wait_recv()
        idx_copy(z, isend.at[0], other).wait_send()

        def fill(s, carry):
            rows = lax.broadcasted_iota(jnp.int32, (tok, tok), 0) + s * tok
            for k in range(4):
                hit = idxv[k][0:1, :] == rows
                select[pl.ds(pl.multiple_of(s * tok, tok), tok), k * tok:(k + 1) * tok] = jnp.where(
                    hit, 1.0, 0.0
                ).astype(jnp.bfloat16)
            return carry

        lax.fori_loop(0, 4, fill, 0)
        for n in range(4):
            c_copy(0, n, across, across).wait_recv()
            c_copy(2, n, across, sibling).start()

        def hand_on(j):
            u_copy(leaf, j, usend.at[1, j], other).wait_recv()
            u_copy(leaf, j, usend.at[1, j], other).start()

        for n in range(4):
            c_copy(1, n, sibling, sibling).wait_recv()
        for n in range(4):
            c_copy(2, n, across_sibling, sibling).wait_recv()

        def by_slot(k, carry):
            st[k // 2, pl.ds(pl.multiple_of(lax.rem(k, 2) * share, share), share), :] = lax.dot_general(
                cbuf[k], select[...], (((0,), (1,)), ((), ())), preferred_element_type=jnp.float32
            ).astype(jnp.bfloat16)
            for step in range(chunks // 4):
                hand_on(k * (chunks // 4) + step)
            return carry

        lax.fori_loop(0, 4, by_slot, 0)

        def finish(j, carry):
            u_copy(other, j, usend.at[0, j], other).wait_recv()
            u_copy(far_leaf, j, usend.at[0, j], other).wait_recv()
            part = uall[:, :, cols(j)].reshape(4 * tok, CHUNK)
            stage[:, cols(j)] = jnp.dot(st[z - 1], part, preferred_element_type=jnp.float32).astype(jnp.bfloat16)
            g_copy(j, leaf).start()
            outv[:, cols(j)] = jnp.dot(st[2 - z], part, preferred_element_type=jnp.float32)
            out_copy(j).start()
            return carry

        lax.fori_loop(0, chunks, finish, 0)
        for n in range(4):
            c_copy(0, n, c, across).wait_send()
            c_copy(1, n, c, sibling).wait_send()
            c_copy(2, n, across, sibling).wait_send()
        for j in range(chunks):
            u_copy(z, j, usend.at[0, j], other).wait_send()
            u_copy(leaf, j, usend.at[1, j], other).wait_send()
            g_copy(j, leaf).wait_send()
            out_copy(j).wait()


def line_body(feature_cache, owner_ids, slot_ids, live_tokens, tap_gain, key_cotangent, value_cotangent):
    owned, block_len, _, columns = feature_cache.shape
    tok, share = key_cotangent.shape
    chunks = columns // CHUNK
    z = lax.axis_index("dp")
    near = lax.ppermute(jnp.where((z == 0), key_cotangent, value_cotangent), "dp", [(0, 1), (3, 2)])
    mid = lax.ppermute(jnp.where((z == 2), key_cotangent, value_cotangent), "dp", [(1, 2), (2, 1)])
    far = lax.ppermute(jnp.where((z == 3), key_cotangent, value_cotangent), "dp", [(0, 2), (3, 1)])
    mine = jnp.where(z == 1, key_cotangent, value_cotangent)
    offsets = jnp.arange(block_len, dtype=jnp.int32)
    first = (owner_ids[:, 0] * owned + slot_ids) * block_len
    index = jnp.where(offsets[None, :] < live_tokens[:, None], first[:, None] + offsets[None, :], -1)
    index = jnp.broadcast_to(index.reshape(1, tok), (8, tok))
    united = united_of(feature_cache, tap_gain, columns * lax.axis_size("tensor")).reshape(tok, columns)
    anywhere = pl.BlockSpec(memory_space=pl.ANY)
    dma = pltpu.SemaphoreType.DMA
    return pl.pallas_call(
        line_kernel,
        out_shape=jax.ShapeDtypeStruct((tok, columns), jnp.float32),
        in_specs=[anywhere] * 6,
        out_specs=anywhere,
        scratch_shapes=[
            pltpu.VMEM((4, tok, columns), jnp.bfloat16),
            pltpu.VMEM((4, 4 * tok, share), jnp.bfloat16),
            pltpu.VMEM((4 * tok, 4 * tok), jnp.bfloat16),
            pltpu.VMEM((2, 2 * share, 4 * tok), jnp.bfloat16),
            pltpu.VMEM((tok, columns), jnp.bfloat16),
            pltpu.VMEM((tok, columns), jnp.bfloat16),
            pltpu.VMEM((tok, columns), jnp.float32),
            pltpu.VMEM((4, 8, tok), jnp.int32),
            dma((2, chunks)), dma((4, chunks)), dma((3, 4)), dma((3, 4)),
            dma((chunks,)), dma((chunks,)), dma((chunks,)), dma((6,)), dma((2,)), dma((4,)),
        ],
        compiler_params=pltpu.CompilerParams(
            collective_id=0, has_side_effects=True, vmem_limit_bytes=56 * 1024 * 1024
        ),
    )(united, index, mine, near, mid, far)


def solution(mesh):
    in_specs = (
        P(("groups", "dp"), None, None, "tensor"),
        P(("groups", "dp"), None),
        P(("groups", "dp")),
        P(("groups", "dp")),
        P(None, "tensor"),
        P(("groups", "dp"), "tensor"),
        P(("groups", "dp"), "tensor"),
    )
    body = line_body if mesh.shape["dp"] == 4 and mesh.shape["tensor"] == 4 else general_body
    out_specs = P(("groups", "dp"), "tensor")
    return jax.shard_map(body, mesh=mesh, in_specs=in_specs, out_specs=out_specs, check_vma=False)
```

```python
import jax
import jax.numpy as jnp
from jax import lax
from jax.experimental import pallas as pl
from jax.experimental.pallas import tpu as pltpu
from jax.sharding import PartitionSpec as P

EPSILON = 1e-06


def united_of(feature_cache, tap_gain, width):
    floats = feature_cache.astype(jnp.float32)
    squares = lax.psum(jnp.sum(floats * floats, axis=-1), "tensor")
    inverse_rms = lax.rsqrt(squares / width + EPSILON)
    return jnp.sum(floats * inverse_rms[..., None] * tap_gain, axis=2).astype(jnp.bfloat16)


def slot_matrix(owner_ids, slot_ids, live_tokens, owned, dtype):
    index = owner_ids[:, 0] * owned + slot_ids
    table = lax.all_gather(jnp.stack([index, live_tokens]), "dp", axis=1, tiled=True)
    slots = lax.axis_size("dp") * owned
    chosen = jnp.arange(slots, dtype=jnp.int32)[:, None] == table[0][None, :]
    return chosen.astype(dtype), table[1]


def general_body(feature_cache, owner_ids, slot_ids, live_tokens, tap_gain, key_cotangent, value_cotangent):
    owned, block_len, _, columns = feature_cache.shape
    width = columns * lax.axis_size("tensor")
    united = united_of(feature_cache, tap_gain, width).reshape(owned * block_len, columns)
    everywhere = lax.all_gather(united, "dp", axis=0, tiled=True)
    chosen, live = slot_matrix(owner_ids, slot_ids, live_tokens, owned, jnp.bfloat16)
    joined = jnp.concatenate(
        [
            lax.all_gather(key_cotangent, "tensor", axis=1, tiled=True),
            lax.all_gather(value_cotangent, "tensor", axis=1, tiled=True),
        ],
        axis=1,
    )
    mine = lax.all_to_all(joined, "dp", split_axis=1, concat_axis=0, tiled=True)
    rows = mine.shape[1]
    mine = mine.reshape(-1, block_len, rows)
    mask = jnp.arange(block_len, dtype=jnp.int32)[None, :] < live[:, None]
    mine = jnp.where(mask[:, :, None], mine, jnp.zeros_like(mine)).reshape(-1, block_len * rows)
    by_slot = lax.dot_general(
        chosen, mine, (((1,), (0,)), ((), ())), preferred_element_type=jnp.float32
    ).astype(jnp.bfloat16).reshape(-1, rows)
    return lax.dot_general(
        by_slot, everywhere, (((0,), (0,)), ((), ())), preferred_element_type=jnp.float32
    )


MESH = pl.DeviceIdType.MESH
CHUNK = 256


def line_kernel(
    f_in, gain_in, idx_in, key_in, value_in, out,
    fv, gain, sums, scale, uall, cbuf, select, st, gbuf, stage, idxv,
    usend, urecv, csend, crecv, gsend, grecv, osem, lsem, isend, irecv, fsem, zsend, zrecv, ssend, srecv,
):
    z, c = lax.axis_index("dp"), lax.axis_index("tensor")
    owned, taps, block_len, columns = f_in.shape
    tok, share = key_in.shape
    chunks = columns // CHUNK
    groups = fsem.shape[0]
    group = owned // groups
    sibling, across = c + 1 - 2 * lax.rem(c, 2), lax.rem(c + 2, 4)
    across_sibling = lax.rem(sibling + 2, 4)
    is_hub = (z == 1) | (z == 2)

    def remote(src, dst, ss, rs, dz, dc):
        return pltpu.make_async_remote_copy(
            src_ref=src, dst_ref=dst, send_sem=ss, recv_sem=rs,
            device_id={"dp": dz, "tensor": dc}, device_id_type=MESH,
        )

    def cols(j):
        return pl.ds(pl.multiple_of(j * CHUNK, CHUNK), CHUNK)

    def place(owner):
        return pl.ds(pl.multiple_of(owner * tok, tok), tok)

    def f_copy(g):
        part = pl.ds(g * group, group)
        return pltpu.make_async_copy(f_in.at[part], fv.at[part], fsem.at[g])

    own_idx = pltpu.make_async_copy(idx_in, idxv.at[z], lsem.at[1])
    own_gain = pltpu.make_async_copy(gain_in, gain, lsem.at[2])
    for g in range(groups):
        f_copy(g).start()
    own_idx.start()
    own_gain.start()

    @pl.when(z == 1)
    def _():
        pltpu.make_async_copy(key_in, cbuf.at[c, place(1)], lsem.at[0]).start()

    @pl.when(z == 2)
    def _():
        pltpu.make_async_copy(value_in, cbuf.at[c, place(2)], lsem.at[0]).start()

    barrier = pltpu.get_barrier_semaphore()
    for step in range(1, 4):
        pl.semaphore_signal(
            barrier, inc=1, device_id={"dp": lax.rem(z + step, 4), "tensor": c}, device_id_type=MESH
        )
    for step in range(1, 4):
        pl.semaphore_signal(
            barrier, inc=1, device_id={"dp": z, "tensor": lax.rem(c + step, 4)}, device_id_type=MESH
        )
    pl.semaphore_wait(barrier, 6)

    def u_copy(owner, j, sem, dz):
        return remote(uall.at[owner, :, cols(j)], uall.at[owner, :, cols(j)], sem, urecv.at[owner, j], dz, c)

    def idx_copy(owner, sem, dz):
        return remote(idxv.at[owner], idxv.at[owner], sem, irecv.at[owner], dz, c)

    def g_copy(j, dz):
        return remote(stage.at[:, cols(j)], gbuf.at[:, cols(j)], gsend.at[j], grecv.at[j], dz, c)

    def z_copy(ref, n, owner, dz):
        return remote(ref, cbuf.at[c, place(owner)], zsend.at[n], zrecv.at[owner], dz, c)

    def c_copy(kind, owner, who, dc):
        part = cbuf.at[who, place(owner)]
        return remote(part, part, csend.at[kind, owner], crecv.at[kind, owner], z, dc)

    def s_copy(owner, step):
        return remote(
            sums.at[owner], sums.at[owner], ssend.at[step - 1], srecv.at[owner], z, lax.rem(c + step, 4)
        )

    @pl.when(z != 1)
    def _():
        z_copy(key_in, 0, z, 1).start()

    @pl.when(z != 2)
    def _():
        z_copy(value_in, 1, z, 2).start()

    own_idx.wait()

    @pl.when(is_hub)
    def _():
        idx_copy(z, isend.at[0], 3 - z).start()
        pltpu.make_async_copy(key_in, cbuf.at[c, place(z)], lsem.at[0]).wait()
        c_copy(0, z, c, across).start()
        c_copy(1, z, c, sibling).start()

    @pl.when(jnp.logical_not(is_hub))
    def _():
        for n in range(2):
            idx_copy(z, isend.at[n], 1 + n).start()

    width = sums.shape[2]
    lanes = lax.broadcasted_iota(jnp.int32, (block_len, width), 1)
    total = jnp.zeros((block_len, width), jnp.float32)
    for g in range(groups):
        f_copy(g).wait()

        def squares(i, acc, g=g):
            b = g * group + i
            x = fv[b].astype(jnp.float32)
            row = jnp.sum(x * x, axis=-1, keepdims=True)
            for t in range(taps):
                acc = jnp.where(lanes == b * taps + t, row[t], acc)
            return acc

        total = lax.fori_loop(0, group, squares, total, unroll=2)
    sums[c] = total
    for step in range(1, 4):
        s_copy(c, step).start()
    own_gain.wait()
    for step in range(1, 4):
        s_copy(lax.rem(c + step, 4), step).wait_recv()
    inverse = lax.rsqrt((sums[0] + sums[1] + sums[2] + sums[3]) / (4 * columns) + EPSILON)

    def spread(k, carry):
        one = jnp.sum(jnp.where(lanes == k, inverse, 0.0), axis=-1, keepdims=True)
        scale[k] = jnp.broadcast_to(one, (block_len, 128))
        return carry

    lax.fori_loop(0, owned * taps, spread, 0, unroll=8)

    target = 1 + lax.rem(z, 2)

    def unite(j, carry):
        gains = [jnp.broadcast_to(gain[t:t + 1, cols(j)], (block_len, CHUNK)) for t in range(taps)]

        def pair(i, inner):
            rows = []
            for d in range(2):
                b = 2 * i + d
                row = jnp.zeros((block_len, CHUNK), jnp.float32)
                for t in range(taps):
                    s = scale[b * taps + t]
                    s = jnp.concatenate([s] * (CHUNK // 128), axis=-1)
                    row = row + fv[b, t, :, cols(j)].astype(jnp.float32) * s * gains[t]
                rows.append(row)
            where = pl.ds(pl.multiple_of(i * 2 * block_len, 2 * block_len), 2 * block_len)
            uall[z, where, cols(j)] = jnp.concatenate(rows, axis=0).astype(jnp.bfloat16)
            return inner

        lax.fori_loop(0, owned // 2, pair, 0, unroll=4)
        u_copy(z, j, usend.at[0, j], target).start()
        return carry

    lax.fori_loop(0, chunks, unite, 0)

    @pl.when(jnp.logical_not(is_hub))
    def _():
        def out_copy(j):
            return pltpu.make_async_copy(gbuf.at[:, cols(j)], out.at[:, cols(j)], osem.at[j])

        def take(j, carry):
            g_copy(j, target).wait_recv()
            out_copy(j).start()
            return carry

        lax.fori_loop(0, chunks, take, 0)
        for n in range(2):
            idx_copy(z, isend.at[n], 1 + n).wait_send()
        for j in range(chunks):
            out_copy(j).wait()

    @pl.when(is_hub)
    def _():
        leaf, other = 3 * (z - 1), 3 - z
        far_leaf = 3 - leaf
        guests = (leaf, other, far_leaf)

        def out_copy(j):
            return pltpu.make_async_copy(gbuf.at[:, cols(j)], out.at[:, cols(j)], osem.at[j])

        for owner in guests:
            z_copy(key_in, 0, owner, other).wait_recv()
            c_copy(0, owner, c, across).start()
            c_copy(1, owner, c, sibling).start()
        for owner in guests:
            idx_copy(owner, isend.at[0], other).wait_recv()

        def fill(s, carry):
            rows = lax.broadcasted_iota(jnp.int32, (tok, tok), 0) + s * tok
            for k in range(4):
                hit = idxv[k][0:1, :] == rows
                select[place(s), k * tok:(k + 1) * tok] = jnp.where(hit, 1.0, 0.0).astype(jnp.bfloat16)
            return carry

        lax.fori_loop(0, 4, fill, 0)
        for owner in (z,) + guests:
            c_copy(0, owner, across, across).wait_recv()
            c_copy(2, owner, across, sibling).start()

        def hand_on(j):
            u_copy(leaf, j, usend.at[1, j], other).wait_recv()
            u_copy(leaf, j, usend.at[1, j], other).start()

        for owner in range(4):
            c_copy(1, owner, sibling, sibling).wait_recv()
        for owner in range(4):
            c_copy(2, owner, across_sibling, sibling).wait_recv()

        def by_slot(k, carry):
            st[k // 2, pl.ds(pl.multiple_of(lax.rem(k, 2) * share, share), share), :] = lax.dot_general(
                cbuf[k], select[...], (((0,), (1,)), ((), ())), preferred_element_type=jnp.float32
            ).astype(jnp.bfloat16)
            for step in range(chunks // 4):
                hand_on(k * (chunks // 4) + step)
            return carry

        lax.fori_loop(0, 4, by_slot, 0)

        def finish(j, carry):
            u_copy(other, j, usend.at[0, j], other).wait_recv()
            u_copy(far_leaf, j, usend.at[0, j], other).wait_recv()
            part = uall[:, :, cols(j)].reshape(4 * tok, CHUNK)
            stage[:, cols(j)] = jnp.dot(st[z - 1], part, preferred_element_type=jnp.float32).astype(jnp.bfloat16)
            g_copy(j, leaf).start()
            gbuf[:, cols(j)] = jnp.dot(st[2 - z], part, preferred_element_type=jnp.float32).astype(jnp.bfloat16)
            out_copy(j).start()
            return carry

        lax.fori_loop(0, chunks, finish, 0)
        idx_copy(z, isend.at[0], other).wait_send()
        for owner in range(4):
            c_copy(0, owner, c, across).wait_send()
            c_copy(1, owner, c, sibling).wait_send()
            c_copy(2, owner, across, sibling).wait_send()
        for j in range(chunks):
            u_copy(leaf, j, usend.at[1, j], other).wait_send()
            g_copy(j, leaf).wait_send()
            out_copy(j).wait()

    for step in range(1, 4):
        s_copy(c, step).wait_send()
    for j in range(chunks):
        u_copy(z, j, usend.at[0, j], target).wait_send()

    @pl.when(z != 1)
    def _():
        z_copy(key_in, 0, z, 1).wait_send()

    @pl.when(z != 2)
    def _():
        z_copy(value_in, 1, z, 2).wait_send()


def line_body(feature_cache, owner_ids, slot_ids, live_tokens, tap_gain, key_cotangent, value_cotangent):
    owned, block_len, taps, columns = feature_cache.shape
    tok, share = key_cotangent.shape
    chunks = columns // CHUNK
    offsets = jnp.arange(block_len, dtype=jnp.int32)
    first = (owner_ids[:, 0] * owned + slot_ids) * block_len
    index = jnp.where(offsets[None, :] < live_tokens[:, None], first[:, None] + offsets[None, :], -1)
    index = jnp.broadcast_to(index.reshape(1, tok), (8, tok))
    features = jnp.transpose(feature_cache, (0, 2, 1, 3))
    anywhere = pl.BlockSpec(memory_space=pl.ANY)
    dma = pltpu.SemaphoreType.DMA
    wide = -(-owned * taps // 128) * 128
    result = pl.pallas_call(
        line_kernel,
        out_shape=jax.ShapeDtypeStruct((tok, columns), jnp.bfloat16),
        in_specs=[anywhere] * 5,
        out_specs=anywhere,
        scratch_shapes=[
            pltpu.VMEM((owned, taps, block_len, columns), jnp.bfloat16),
            pltpu.VMEM((taps, columns), jnp.float32),
            pltpu.VMEM((4, block_len, wide), jnp.float32),
            pltpu.VMEM((owned * taps, block_len, 128), jnp.float32),
            pltpu.VMEM((4, tok, columns), jnp.bfloat16),
            pltpu.VMEM((4, 4 * tok, share), jnp.bfloat16),
            pltpu.VMEM((4 * tok, 4 * tok), jnp.bfloat16),
            pltpu.VMEM((2, 2 * share, 4 * tok), jnp.bfloat16),
            pltpu.VMEM((tok, columns), jnp.bfloat16),
            pltpu.VMEM((tok, columns), jnp.bfloat16),
            pltpu.VMEM((4, 8, tok), jnp.int32),
            dma((2, chunks)), dma((4, chunks)), dma((3, 4)), dma((3, 4)),
            dma((chunks,)), dma((chunks,)), dma((chunks,)), dma((3,)), dma((2,)), dma((4,)),
            dma((8,)), dma((2,)), dma((4,)), dma((3,)), dma((4,)),
        ],
        compiler_params=pltpu.CompilerParams(
            collective_id=0, has_side_effects=True, vmem_limit_bytes=58 * 1024 * 1024
        ),
    )(features, tap_gain, index, key_cotangent, value_cotangent)
    return result.astype(jnp.float32)


def solution(mesh):
    in_specs = (
        P(("groups", "dp"), None, None, "tensor"),
        P(("groups", "dp"), None),
        P(("groups", "dp")),
        P(("groups", "dp")),
        P(None, "tensor"),
        P(("groups", "dp"), "tensor"),
        P(("groups", "dp"), "tensor"),
    )
    body = line_body if mesh.shape["dp"] == 4 and mesh.shape["tensor"] == 4 else general_body
    out_specs = P(("groups", "dp"), "tensor")
    return jax.shard_map(body, mesh=mesh, in_specs=in_specs, out_specs=out_specs, check_vma=False)
```

```python
import jax
import jax.numpy as jnp
from jax import lax
from jax.experimental import pallas as pl
from jax.experimental.pallas import tpu as pltpu
from jax.sharding import PartitionSpec as P

EPSILON = 1e-06


def united_of(feature_cache, tap_gain, width):
    floats = feature_cache.astype(jnp.float32)
    squares = lax.psum(jnp.sum(floats * floats, axis=-1), "tensor")
    inverse_rms = lax.rsqrt(squares / width + EPSILON)
    return jnp.sum(floats * inverse_rms[..., None] * tap_gain, axis=2).astype(jnp.bfloat16)


def slot_matrix(owner_ids, slot_ids, live_tokens, owned, dtype):
    index = owner_ids[:, 0] * owned + slot_ids
    table = lax.all_gather(jnp.stack([index, live_tokens]), "dp", axis=1, tiled=True)
    slots = lax.axis_size("dp") * owned
    chosen = jnp.arange(slots, dtype=jnp.int32)[:, None] == table[0][None, :]
    return chosen.astype(dtype), table[1]


def general_body(feature_cache, owner_ids, slot_ids, live_tokens, tap_gain, key_cotangent, value_cotangent):
    owned, block_len, _, columns = feature_cache.shape
    width = columns * lax.axis_size("tensor")
    united = united_of(feature_cache, tap_gain, width).reshape(owned * block_len, columns)
    everywhere = lax.all_gather(united, "dp", axis=0, tiled=True)
    chosen, live = slot_matrix(owner_ids, slot_ids, live_tokens, owned, jnp.bfloat16)
    joined = jnp.concatenate(
        [
            lax.all_gather(key_cotangent, "tensor", axis=1, tiled=True),
            lax.all_gather(value_cotangent, "tensor", axis=1, tiled=True),
        ],
        axis=1,
    )
    mine = lax.all_to_all(joined, "dp", split_axis=1, concat_axis=0, tiled=True)
    rows = mine.shape[1]
    mine = mine.reshape(-1, block_len, rows)
    mask = jnp.arange(block_len, dtype=jnp.int32)[None, :] < live[:, None]
    mine = jnp.where(mask[:, :, None], mine, jnp.zeros_like(mine)).reshape(-1, block_len * rows)
    by_slot = lax.dot_general(
        chosen, mine, (((1,), (0,)), ((), ())), preferred_element_type=jnp.float32
    ).astype(jnp.bfloat16).reshape(-1, rows)
    return lax.dot_general(
        by_slot, everywhere, (((0,), (0,)), ((), ())), preferred_element_type=jnp.float32
    )


MESH = pl.DeviceIdType.MESH
CHUNK = 128


def line_kernel(
    f_in, gain_in, owner_in, slot_in, live_in, key_in, value_in, out,
    fv, gain, sums, scale, uall, cbuf, select, st, gbuf, stage, idxv,
    usend, urecv, csend, crecv, gsend, grecv, osem, lsem, isend, irecv, fsem, zsend, zrecv, ssend, srecv,
):
    z, c = lax.axis_index("dp"), lax.axis_index("tensor")
    owned, taps, block_len, columns = f_in.shape
    tok, share = key_in.shape
    chunks = columns // CHUNK
    groups = fsem.shape[0]
    group = owned // groups
    sibling, across = c + 1 - 2 * lax.rem(c, 2), lax.rem(c + 2, 4)
    across_sibling = lax.rem(sibling + 2, 4)
    is_hub = (z == 1) | (z == 2)

    def remote(src, dst, ss, rs, dz, dc):
        return pltpu.make_async_remote_copy(
            src_ref=src, dst_ref=dst, send_sem=ss, recv_sem=rs,
            device_id={"dp": dz, "tensor": dc}, device_id_type=MESH,
        )

    def cols(j):
        return pl.ds(pl.multiple_of(j * CHUNK, CHUNK), CHUNK)

    def place(owner):
        return pl.ds(pl.multiple_of(owner * tok, tok), tok)

    def f_copy(g):
        part = pl.ds(g * group, group)
        return pltpu.make_async_copy(f_in.at[part], fv.at[part], fsem.at[g])

    own_gain = pltpu.make_async_copy(gain_in, gain, lsem.at[2])
    for g in range(groups):
        f_copy(g).start()
    own_gain.start()

    @pl.when(z == 1)
    def _():
        pltpu.make_async_copy(key_in, cbuf.at[c, place(1)], lsem.at[0]).start()

    @pl.when(z == 2)
    def _():
        pltpu.make_async_copy(value_in, cbuf.at[c, place(2)], lsem.at[0]).start()

    barrier = pltpu.get_barrier_semaphore()
    for step in range(1, 4):
        pl.semaphore_signal(
            barrier, inc=1, device_id={"dp": lax.rem(z + step, 4), "tensor": c}, device_id_type=MESH
        )
    for step in range(1, 4):
        pl.semaphore_signal(
            barrier, inc=1, device_id={"dp": z, "tensor": lax.rem(c + step, 4)}, device_id_type=MESH
        )
    pl.semaphore_wait(barrier, 6)

    def u_copy(owner, j, sem, dz):
        return remote(uall.at[owner, :, cols(j)], uall.at[owner, :, cols(j)], sem, urecv.at[owner, j], dz, c)

    def idx_copy(owner, sem, dz):
        return remote(idxv.at[owner], idxv.at[owner], sem, irecv.at[owner], dz, c)

    def g_copy(j, dz):
        return remote(stage.at[:, cols(j)], gbuf.at[:, cols(j)], gsend.at[j], grecv.at[j], dz, c)

    def z_copy(ref, n, owner, dz):
        return remote(ref, cbuf.at[c, place(owner)], zsend.at[n], zrecv.at[owner], dz, c)

    def c_copy(kind, owner, who, dc):
        part = cbuf.at[who, place(owner)]
        return remote(part, part, csend.at[kind, owner], crecv.at[kind, owner], z, dc)

    def s_copy(owner, step):
        return remote(
            sums.at[owner], sums.at[owner], ssend.at[step - 1], srecv.at[owner], z, lax.rem(c + step, 4)
        )

    @pl.when(z != 1)
    def _():
        z_copy(key_in, 0, z, 1).start()

    @pl.when(z != 2)
    def _():
        z_copy(value_in, 1, z, 2).start()

    listed = owner_in.shape[1]
    sub = lax.broadcasted_iota(jnp.int32, (8, listed), 0)
    entry = owner_in[...] * owned + slot_in[...]
    both = jnp.where(sub == 0, jnp.broadcast_to(entry, (8, listed)), jnp.broadcast_to(live_in[...], (8, listed)))
    start = lax.broadcasted_iota(jnp.int32, (listed, tok), 0) * block_len
    token = lax.broadcasted_iota(jnp.int32, (listed, tok), 1)
    inside = jnp.where((token >= start) & (token < start + block_len), 1.0, 0.0)
    wide = jnp.dot(
        both.astype(jnp.float32), inside, precision=lax.Precision.HIGHEST, preferred_element_type=jnp.float32
    ).astype(jnp.int32)
    offset = lax.rem(lax.broadcasted_iota(jnp.int32, (1, tok), 1), block_len)
    index = jnp.where(offset < wide[1:2], wide[0:1] * block_len + offset, -1)
    idxv[z] = jnp.broadcast_to(index, (8, tok))

    @pl.when(is_hub)
    def _():
        idx_copy(z, isend.at[0], 3 - z).start()
        pltpu.make_async_copy(key_in, cbuf.at[c, place(z)], lsem.at[0]).wait()
        c_copy(0, z, c, across).start()
        c_copy(1, z, c, sibling).start()

    @pl.when(jnp.logical_not(is_hub))
    def _():
        for n in range(2):
            idx_copy(z, isend.at[n], 1 + n).start()

    width = sums.shape[2]
    lanes = lax.broadcasted_iota(jnp.int32, (block_len, width), 1)
    total = jnp.zeros((block_len, width), jnp.float32)
    for g in range(groups):
        f_copy(g).wait()

        def squares(i, acc, g=g):
            b = g * group + i
            x = fv[b].astype(jnp.float32)
            row = jnp.sum(x * x, axis=-1, keepdims=True)
            for t in range(taps):
                acc = jnp.where(lanes == b * taps + t, row[t], acc)
            return acc

        total = lax.fori_loop(0, group, squares, total, unroll=2)
    sums[c] = total
    for step in range(1, 4):
        s_copy(c, step).start()
    own_gain.wait()
    for step in range(1, 4):
        s_copy(lax.rem(c + step, 4), step).wait_recv()
    inverse = lax.rsqrt((sums[0] + sums[1] + sums[2] + sums[3]) / (4 * columns) + EPSILON)

    def spread(k, carry):
        one = jnp.sum(jnp.where(lanes == k, inverse, 0.0), axis=-1, keepdims=True)
        scale[k] = jnp.broadcast_to(one, (block_len, 128))
        return carry

    lax.fori_loop(0, owned * taps, spread, 0, unroll=8)

    target = 1 + lax.rem(z, 2)

    def unite(j, carry):
        gains = [jnp.broadcast_to(gain[t:t + 1, cols(j)], (block_len, CHUNK)) for t in range(taps)]

        def pair(i, inner):
            rows = []
            for d in range(2):
                b = 2 * i + d
                row = jnp.zeros((block_len, CHUNK), jnp.float32)
                for t in range(taps):
                    s = scale[b * taps + t]
                    s = jnp.concatenate([s] * (CHUNK // 128), axis=-1)
                    row = row + fv[b, t, :, cols(j)].astype(jnp.float32) * s * gains[t]
                rows.append(row)
            where = pl.ds(pl.multiple_of(i * 2 * block_len, 2 * block_len), 2 * block_len)
            uall[z, where, cols(j)] = jnp.concatenate(rows, axis=0).astype(jnp.bfloat16)
            return inner

        lax.fori_loop(0, owned // 2, pair, 0, unroll=4)
        u_copy(z, j, usend.at[0, j], target).start()
        return carry

    lax.fori_loop(0, chunks, unite, 0)

    @pl.when(jnp.logical_not(is_hub))
    def _():
        def out_copy(j):
            return pltpu.make_async_copy(gbuf.at[:, cols(j)], out.at[:, cols(j)], osem.at[j])

        def take(j, carry):
            g_copy(j, target).wait_recv()
            out_copy(j).start()
            return carry

        lax.fori_loop(0, chunks, take, 0)
        for n in range(2):
            idx_copy(z, isend.at[n], 1 + n).wait_send()
        for j in range(chunks):
            out_copy(j).wait()

    @pl.when(is_hub)
    def _():
        leaf, other = 3 * (z - 1), 3 - z
        far_leaf = 3 - leaf
        guests = (leaf, other, far_leaf)

        def out_copy(j):
            return pltpu.make_async_copy(gbuf.at[:, cols(j)], out.at[:, cols(j)], osem.at[j])

        for owner in guests:
            z_copy(key_in, 0, owner, other).wait_recv()
            c_copy(0, owner, c, across).start()
            c_copy(1, owner, c, sibling).start()
        for owner in guests:
            idx_copy(owner, isend.at[0], other).wait_recv()

        def fill(s, carry):
            rows = lax.broadcasted_iota(jnp.int32, (tok, tok), 0) + s * tok
            for k in range(4):
                hit = idxv[k][0:1, :] == rows
                select[place(s), k * tok:(k + 1) * tok] = jnp.where(hit, 1.0, 0.0).astype(jnp.bfloat16)
            return carry

        lax.fori_loop(0, 4, fill, 0)
        for owner in (z,) + guests:
            c_copy(0, owner, across, across).wait_recv()
            c_copy(2, owner, across, sibling).start()

        def hand_on(j):
            u_copy(leaf, j, usend.at[1, j], other).wait_recv()
            u_copy(leaf, j, usend.at[1, j], other).start()

        for owner in range(4):
            c_copy(1, owner, sibling, sibling).wait_recv()
        for owner in range(4):
            c_copy(2, owner, across_sibling, sibling).wait_recv()

        def by_slot(k, carry):
            st[k // 2, pl.ds(pl.multiple_of(lax.rem(k, 2) * share, share), share), :] = lax.dot_general(
                cbuf[k], select[...], (((0,), (1,)), ((), ())), preferred_element_type=jnp.float32
            ).astype(jnp.bfloat16)
            for step in range(chunks // 4):
                hand_on(k * (chunks // 4) + step)
            return carry

        lax.fori_loop(0, 4, by_slot, 0)

        def finish(j, carry):
            u_copy(other, j, usend.at[0, j], other).wait_recv()
            u_copy(far_leaf, j, usend.at[0, j], other).wait_recv()
            part = uall[:, :, cols(j)].reshape(4 * tok, CHUNK)
            stage[:, cols(j)] = jnp.dot(st[z - 1], part, preferred_element_type=jnp.float32).astype(jnp.bfloat16)
            g_copy(j, leaf).start()
            gbuf[:, cols(j)] = jnp.dot(st[2 - z], part, preferred_element_type=jnp.float32).astype(jnp.bfloat16)
            out_copy(j).start()
            return carry

        lax.fori_loop(0, chunks, finish, 0)
        idx_copy(z, isend.at[0], other).wait_send()
        for owner in range(4):
            c_copy(0, owner, c, across).wait_send()
            c_copy(1, owner, c, sibling).wait_send()
            c_copy(2, owner, across, sibling).wait_send()
        for j in range(chunks):
            u_copy(leaf, j, usend.at[1, j], other).wait_send()
            g_copy(j, leaf).wait_send()
            out_copy(j).wait()

    for step in range(1, 4):
        s_copy(c, step).wait_send()
    for j in range(chunks):
        u_copy(z, j, usend.at[0, j], target).wait_send()

    @pl.when(z != 1)
    def _():
        z_copy(key_in, 0, z, 1).wait_send()

    @pl.when(z != 2)
    def _():
        z_copy(value_in, 1, z, 2).wait_send()


def line_body(feature_cache, owner_ids, slot_ids, live_tokens, tap_gain, key_cotangent, value_cotangent):
    owned, block_len, taps, columns = feature_cache.shape
    tok, share = key_cotangent.shape
    chunks = columns // CHUNK
    features = jnp.transpose(feature_cache, (0, 2, 1, 3))
    anywhere = pl.BlockSpec(memory_space=pl.ANY)
    dma = pltpu.SemaphoreType.DMA
    wide = -(-owned * taps // 128) * 128
    result = pl.pallas_call(
        line_kernel,
        out_shape=jax.ShapeDtypeStruct((tok, columns), jnp.bfloat16),
        in_specs=[anywhere] * 2 + [pl.BlockSpec(memory_space=pltpu.VMEM)] * 3 + [anywhere] * 2,
        out_specs=anywhere,
        scratch_shapes=[
            pltpu.VMEM((owned, taps, block_len, columns), jnp.bfloat16),
            pltpu.VMEM((taps, columns), jnp.float32),
            pltpu.VMEM((4, block_len, wide), jnp.float32),
            pltpu.VMEM((owned * taps, block_len, 128), jnp.float32),
            pltpu.VMEM((4, tok, columns), jnp.bfloat16),
            pltpu.VMEM((4, 4 * tok, share), jnp.bfloat16),
            pltpu.VMEM((4 * tok, 4 * tok), jnp.bfloat16),
            pltpu.VMEM((2, 2 * share, 4 * tok), jnp.bfloat16),
            pltpu.VMEM((tok, columns), jnp.bfloat16),
            pltpu.VMEM((tok, columns), jnp.bfloat16),
            pltpu.VMEM((4, 8, tok), jnp.int32),
            dma((2, chunks)), dma((4, chunks)), dma((3, 4)), dma((3, 4)),
            dma((chunks,)), dma((chunks,)), dma((chunks,)), dma((3,)), dma((2,)), dma((4,)),
            dma((8,)), dma((2,)), dma((4,)), dma((3,)), dma((4,)),
        ],
        compiler_params=pltpu.CompilerParams(
            collective_id=0, has_side_effects=True, vmem_limit_bytes=58 * 1024 * 1024
        ),
    )(
        features,
        tap_gain,
        owner_ids.reshape(1, -1),
        slot_ids.reshape(1, -1),
        live_tokens.reshape(1, -1),
        key_cotangent,
        value_cotangent,
    )
    return result.astype(jnp.float32)


def solution(mesh):
    in_specs = (
        P(("groups", "dp"), None, None, "tensor"),
        P(("groups", "dp"), None),
        P(("groups", "dp")),
        P(("groups", "dp")),
        P(None, "tensor"),
        P(("groups", "dp"), "tensor"),
        P(("groups", "dp"), "tensor"),
    )
    body = line_body if mesh.shape["dp"] == 4 and mesh.shape["tensor"] == 4 else general_body
    out_specs = P(("groups", "dp"), "tensor")
    return jax.shard_map(body, mesh=mesh, in_specs=in_specs, out_specs=out_specs, check_vma=False)
```
